32 devices in a mesh: group: 4 (over y, x), hash: 8 (over z, core).
Axes of the slice: x: 2, y: 2, z: 4, core: 2. Of those that a mesh axis runs over, the one named last changes fastest.
Arguments:
- pooled: bfloat16 [8, 512, 32, 256], P('hash', 'group'), may hold values from -0.375 to 0.375
- weight: bfloat16 [1024, 2048], replicated, may hold values from -0.1875 to 0.1875
- cotangent: bfloat16 [8, 512, 2048], P('hash', 'group'), may hold values from -6 to 6
- owners: int32 [8, 32, 512, 2], P('hash', 'group'), may hold values from 0 to 7, all different within a row; in each aligned block of 4096 rows (0 to 4095, 4096 to 8191, ..., all dimensions but the last counted through in order) at most 1365 rows name the same one
- local_rows: int32 [8, 32, 512, 2], P('hash', 'group'), may hold values from 0 to 511
- table: float32 [32, 4096, 256], P('group', 'hash'), may hold values from -0.625 to 0.625
- accum: float32 [32, 4096], P('group', 'hash'), may hold values from 0.05 to 2
Outputs:
- wgrad: bfloat16 [1024, 2048], replicated
- table_out: float32 [32, 4096, 256], P('group', 'hash')
- accum_out: float32 [32, 4096], P('group', 'hash')
The draws below stay inside these ranges and needn't reach their ends.
Inputs may be any that keep to these rules, and one draw needn't show every extreme that they name: Among the rows of one device (aligned blocks of 4096 bags), no owner is named more than 1365 times, a bound that some block reaches; the 2 owners of one bag differ.
All inputs are finite; a program needn't handle non-finite values.
Results may differ from the reference program's by a relative error of at most 0.0059.
Values may be sent and summed in bfloat16 or wider, within the bound.
No kernel may reach another device: no remote copies, remote signals or barrier semaphores. Data moves between devices by JAX's collectives and lax.ppermute only.
A program may use at most 128 MiB of HBM per device.

```python
import math
import jax
import jax.numpy as jnp
import numpy as np
from jax import lax

E = 256
H = 2048
FEATS = 32
L = 2
S_DEV = 128
ROWS_DEV = 512
PAIRS = 1024
SAMPLES = 4096
CAP = 1365
N_GROUP = 4
N_HASH = 8


def with_ends(array, key, least, largest):
    place = [jax.random.randint(jax.random.fold_in(key, axis), (), 0, length) for axis, length in enumerate(array.shape)]
    main_axis = array.shape.index(max(array.shape))
    neighbour = place[:main_axis] + [(place[main_axis] + 1) % array.shape[main_axis]] + place[main_axis + 1:]
    return array.at[tuple(place)].set(least).at[tuple(neighbour)].set(largest)


def levels(own_key, extent, pieces, low, top_value):
    def one(axis_at, shards_of):
        steps = jax.random.uniform(jax.random.fold_in(jax.random.fold_in(own_key, 6), axis_at), (shards_of,), jnp.float32, low / len(pieces), top_value / len(pieces))
        return jnp.repeat(jnp.exp(steps), extent[axis_at] // shards_of).reshape((-1,) + (1,) * (len(extent) - axis_at - 1))

    loudness = one(*pieces[0])
    for cut in pieces[1:]:
        loudness = loudness * one(*cut)
    return loudness


def cumulative_ranks(number_of, slope):
    loads = [(1 << 20) // math.isqrt(rank ** slope) + 1 for rank in range(1, number_of + 1)]
    width = 1 + sum(loads) // (1 << 30)
    return np.cumsum(np.array([max(1, weight // width) for weight in loads]))


def skewed_ids(stream_key, shape, amount, skew):
    listing = cumulative_ranks(amount, skew)
    pick = jax.random.randint(jax.random.fold_in(stream_key, 1), shape, 0, int(listing[amount - 1]))
    rank = jnp.searchsorted(jnp.asarray(listing, jnp.int32), pick, side="right")
    return jax.random.permutation(jax.random.fold_in(stream_key, 2), amount)[rank].astype(jnp.int32)


def shared_out(own_key, own, number, rows, count, top, most, lean):
    order = jax.random.permutation(own_key, count)
    heavy_load, ordinary = portions_of(count, rows * top, most, lean, True), portions_of(count, rows * top, most, lean, False)
    places = jnp.arange(count)

    def named(tallies, rotation):
        used = int((tallies > 0).sum())
        fixed = max(1, used // 4)
        shifted = fixed + (places - fixed + rotation * (used - fixed)) % max(1, count - fixed)
        return jnp.zeros((count,), jnp.int32).at[order[jnp.where(places < fixed, places, shifted)]].set(jnp.asarray(tallies, jnp.int32))

    tallies = jnp.where(number % 4 == 0, named(heavy_load, number // 4), named(ordinary, number - number // 4 - 1))
    mixed = jax.random.permutation(jax.random.fold_in(own, 3), count)
    giver, sink = mixed[0:count // 2 * 2:2], mixed[1:count // 2 * 2:2]
    margin = jnp.minimum(tallies[giver] - 1, most - tallies[sink]) // 2
    margin = jnp.where((giver == order[0]) | (sink == order[0]) | (tallies[sink] == 0), 0, jnp.maximum(margin, 0))
    shifted = jax.random.randint(jax.random.fold_in(own, 4), (count // 2,), 0, 1 << 20) % (margin + 1)
    tallies = tallies.at[giver].add(-shifted).at[sink].add(shifted)
    items = jnp.searchsorted(jnp.cumsum(tallies), jnp.arange(rows * top), side="right").astype(jnp.int32)
    listing = items.reshape(top, rows).T
    listing = listing[jax.random.permutation(jax.random.fold_in(own, 1), rows)]
    rotation = jax.random.randint(jax.random.fold_in(own, 2), (rows, 1), 0, top)
    return jnp.take_along_axis(listing, (jnp.arange(top)[None, :] + rotation) % top, axis=1)


def portions_of(count, total, reach, lean, full):
    loads = [(1 << 20) // math.isqrt(standing ** lean) + 1 for standing in range(1, count + 1)]
    largest = reach if full else min(reach, max(-(-total // count), total * loads[0] // sum(loads)))
    least = 1 if total - largest >= count - 1 else 0
    counts, surplus = [largest] + [least] * (count - 1), total - largest - least * (count - 1)
    while surplus > 0:
        movable = [i for i in range(1, count) if counts[i] < largest] or [i for i in range(1, count) if counts[i] < reach]
        whole, budget = sum([loads[i] for i in movable]), surplus
        for i in movable:
            extra = min(reach - counts[i], max(1, budget * loads[i] // whole), surplus)
            counts[i] = counts[i] + extra
            surplus = surplus - extra
    return np.array(counts)


def bell_draw(own_key, dims, spread, limit, pieces=(), kind=jnp.bfloat16):
    array = jax.random.normal(own_key, dims, jnp.float32) * spread
    if len(pieces) > 0:
        array = levels(own_key, dims, pieces, -0.22, 0.18) * array
    return jnp.clip(array, min=-limit, max=limit).astype(kind)


def setup_inputs(seed: int = 0) -> dict:
    key_list = jax.random.split(jax.random.key(seed), 8)
    pooled = bell_draw(key_list[0], (N_HASH, N_GROUP * S_DEV, FEATS, E), 0.0625, 0.375, ((0, 8), (1, 4)))
    weight = bell_draw(key_list[1], (PAIRS, H), PAIRS ** -0.5, 0.1875)
    cotangent = bell_draw(key_list[2], (N_HASH, N_GROUP * S_DEV, H), 1.0, 6.0, ((0, 8), (1, 4)))
    owners_keys = jax.random.split(jax.random.fold_in(key_list[3], 1), N_HASH * FEATS * (N_GROUP * S_DEV) // (FEATS * S_DEV))
    owners_turns = jax.random.permutation(jax.random.fold_in(key_list[3], 3), N_HASH * FEATS * (N_GROUP * S_DEV) // (FEATS * S_DEV))
    owners = jax.vmap(lambda own, number: shared_out(jax.random.fold_in(key_list[3], 2), own, number, FEATS * S_DEV, N_HASH, L, CAP, 1))(owners_keys, owners_turns).reshape((N_HASH, FEATS, N_GROUP * S_DEV, L))
    local_rows = with_ends(skewed_ids(key_list[4], (N_HASH, FEATS, N_GROUP * S_DEV, L), ROWS_DEV, 2), jax.random.fold_in(key_list[4], 3), 0, ROWS_DEV - 1).astype(jnp.int32)
    table = bell_draw(key_list[5], (FEATS, N_HASH * ROWS_DEV, E), 0.1, 0.625, ((0, 4), (1, 8)), jnp.float32)
    accum = jnp.clip(jnp.exp(math.log(2.0) - 3.6888794 * jax.random.uniform(key_list[6], (FEATS, N_HASH * ROWS_DEV), jnp.float32) ** levels(key_list[6], (FEATS, N_HASH * ROWS_DEV), ((0, 4), (1, 8)), -0.2, 0.2)), 0.05, 2.0)
    return dict(pooled=pooled, weight=weight, cotangent=cotangent, owners=owners, local_rows=local_rows, table=table, accum=accum)


def reference(pooled, weight, cotangent, owners, local_rows, table, accum):

    def step(carry, inputs):
        wsum, rsum = carry
        vectors, cotan, owner_block, row_block = inputs
        count = vectors.shape[0]
        inter = jnp.einsum('sfe,sge->sfg', vectors.astype(jnp.float32), vectors.astype(jnp.float32)).astype(jnp.bfloat16)
        inter_rows = inter.reshape(count, FEATS * FEATS)
        preact = jnp.dot(inter_rows, weight, preferred_element_type=jnp.float32)
        sigmoid_v = jax.nn.sigmoid(preact)
        dpre = (cotan.astype(jnp.float32) * (sigmoid_v * (1.0 + preact * (1.0 - sigmoid_v)))).astype(jnp.bfloat16)
        wsum = wsum + lax.dot_general(inter_rows, dpre, (((0,), (0,)), ((), ())), preferred_element_type=jnp.float32)
        dinter = lax.dot_general(dpre, weight, (((1,), (1,)), ((), ())), preferred_element_type=jnp.float32).reshape(count, FEATS, FEATS)
        dsym = (dinter + jnp.swapaxes(dinter, 1, 2)).astype(jnp.bfloat16)
        dpooled = jnp.einsum('sfg,sge->fse', dsym.astype(jnp.float32), vectors.astype(jnp.float32)).astype(jnp.bfloat16)
        keys = (owner_block * ROWS_DEV + row_block).astype(jnp.int32)
        values = jnp.broadcast_to(dpooled[:, :, None, :].astype(jnp.float32), keys.shape + (E,))

        def one_feature(vals, feature_keys):
            return jax.ops.segment_sum(vals.reshape(-1, E), feature_keys.reshape(-1), num_segments=N_HASH * ROWS_DEV)
        rsum = rsum + jax.vmap(one_feature)(values, keys)
        return ((wsum, rsum), None)
    start = (jnp.zeros((FEATS * FEATS, H), jnp.float32), jnp.zeros((FEATS, N_HASH * ROWS_DEV, E), jnp.float32))
    (wsum, rowgrad), _ = lax.scan(step, start, (pooled, cotangent, owners, local_rows))
    wgrad = (wsum / math.sqrt(SAMPLES)).astype(jnp.bfloat16)
    accum_out = accum + lax.optimization_barrier(jnp.mean(rowgrad * rowgrad, axis=-1))
    table_out = table - 0.1 * rowgrad / jnp.sqrt(accum_out)[:, :, None]
    return (wgrad, table_out, accum_out)
```

```python
import functools
import math

import jax
import jax.numpy as jnp
from jax import lax
from jax.experimental import pallas as pl
from jax.experimental.pallas import tpu as pltpu
from jax.sharding import PartitionSpec as P


def chunk_sizes(feats_local):
    if feats_local < 4 or feats_local % 4:
        return [1] * feats_local
    step = feats_local // 4
    if step % 2:
        return [step] * 4
    return [step] * 2 + [step + step // 2, step // 2]


def pair_table(feats):
    half = feats // 2
    first = [f * feats + g for f in range(half) for g in range(f, half)]
    second = [f * feats + g for f in range(half, feats) for g in range(f, feats)]
    mixed = [f * feats + g for f in range(half) for g in range(half, feats)]
    spare = [-1] * (-len(first) % 16)
    return first + spare + mixed + spare + second


def rows_kernel(sets, keys_ref, *refs):
    vec_refs, (own_ref, sib_ref) = refs[:-2], refs[-2:]
    rows, width = own_ref.shape[1:]
    samples = keys_ref.shape[-1]
    row_id = lax.broadcasted_iota(jnp.int32, (rows, samples), 0)
    vectors = [
        jnp.concatenate([vec_refs[i][:, 0].reshape(-1, width) for i in members], axis=0) for members in sets
    ]
    for target, out_ref in enumerate((own_ref, sib_ref)):
        total = jnp.zeros((rows, width), jnp.float32)
        for line, vec in enumerate(vectors):
            key = keys_ref[target, 0, line : line + 1, :]
            hit = jnp.where(row_id == key, 1.0, 0.0).astype(jnp.bfloat16)
            total = total + jnp.dot(hit, vec, preferred_element_type=jnp.float32)
        out_ref[0] = total.astype(out_ref.dtype)


def dense_rows(keys, sets, vectors, starts, first, feats, rows):
    width = vectors[0].shape[-1]

    def vec_spec(value, start):
        return pl.BlockSpec((value.shape[0], 1) + value.shape[2:], lambda f: (0, start + f, 0, 0))

    key_spec = pl.BlockSpec((2, 1) + keys.shape[2:], lambda f: (0, first + f, 0, 0))
    out_spec = pl.BlockSpec((1, rows, width), lambda f: (f, 0, 0))
    samples = keys.shape[2] * keys.shape[3]
    return pl.pallas_call(
        functools.partial(rows_kernel, sets),
        grid=(feats,),
        in_specs=[key_spec] + [vec_spec(value, start) for value, start in zip(vectors, starts)],
        out_specs=[out_spec, out_spec],
        out_shape=[
            jax.ShapeDtypeStruct((feats, rows, width), jnp.float32),
            jax.ShapeDtypeStruct((feats, rows, width), jnp.bfloat16),
        ],
        cost_estimate=pl.CostEstimate(
            flops=4 * feats * rows * samples * width,
            bytes_accessed=feats * width * (2 * samples + 6 * rows),
            transcendentals=0,
        ),
        name="dense_rows",
    )(keys, *vectors)


def update_kernel(sizes, first, *refs):
    count = len(sizes)
    own_refs, other_refs = refs[:count], refs[count : 2 * count]
    table_ref, accum_ref, before_ref = refs[2 * count : 2 * count + 3]
    table_out, accum_out = refs[-2:]
    rows, width = table_ref.shape[1:]
    lanes = 128
    step = pl.program_id(0)

    @pl.when(step == 0)
    def _():
        accum_out[...] = before_ref[...]

    def one(own_ref, other_ref):
        grad = own_ref[0] + other_ref[0].astype(jnp.float32)
        square = grad * grad
        part = square[:, :lanes]
        for start in range(lanes, width, lanes):
            part = part + square[:, start : start + lanes]
        mean = jnp.sum(part.T, axis=0, keepdims=True) * (1.0 / width)
        line = pl.ds(first + step, 1)
        state = accum_ref[line, :] + mean
        accum_out[line, :] = state
        scale = jnp.broadcast_to(0.1 / jnp.sqrt(state), (lanes, rows)).T
        for start in range(0, width, lanes):
            window = pl.ds(start, lanes)
            table_out[0, :, window] = table_ref[0, :, window] - grad[:, start : start + lanes] * scale

    low = 0
    for size, own_ref, other_ref in zip(sizes, own_refs, other_refs):
        pl.when((step >= low) & (step < low + size))(functools.partial(one, own_ref, other_ref))
        low += size


def update(owns, others, table, accum, first, before):
    sizes = [own.shape[0] for own in owns]
    rows, width = owns[0].shape[1:]
    feats = sum(sizes)

    def part(low, size):
        return pl.BlockSpec((1, rows, width), lambda f: (jnp.clip(f - low, 0, size - 1), 0, 0))

    parts, low = [], 0
    for size in sizes:
        parts.append(part(low, size))
        low += size
    whole = pl.BlockSpec((1, rows, width), lambda f: (first + f, 0, 0))
    lines = pl.BlockSpec(accum.shape, lambda f: (0, 0))
    extra = [] if before is None else [before[0]]
    return pl.pallas_call(
        functools.partial(update_kernel, sizes, first),
        grid=(feats,),
        in_specs=parts + parts + [whole, lines, lines] + [pl.BlockSpec(memory_space=pl.ANY)] * len(extra),
        out_specs=[whole, lines],
        out_shape=[
            jax.ShapeDtypeStruct(table.shape, table.dtype),
            jax.ShapeDtypeStruct(accum.shape, accum.dtype),
        ],
        input_output_aliases={2 * len(owns) + 3: 0} if extra else {},
        cost_estimate=pl.CostEstimate(
            flops=8 * feats * rows * width,
            bytes_accessed=14 * feats * rows * width,
            transcendentals=feats * rows,
        ),
        name="update_rows",
    )(*owns, *others, table, accum, accum if before is None else before[1], *extra)


def unpack_kernel(core_ref, place_ref, mine_ref, theirs_ref, out_ref):
    parts, pairs, depth = place_ref.shape
    rows, cols = mine_ref.shape[1:]
    low = core_ref[0] == 0
    mine, theirs = mine_ref[0], theirs_ref[0]
    for end, block in enumerate((jnp.where(low, mine, theirs), jnp.where(low, theirs, mine))):
        for part in range(parts):
            start = part * (rows - depth)
            out = jnp.dot(
                place_ref[part], block[start : start + depth], preferred_element_type=jnp.float32
            )
            out_ref[pl.ds(part * pairs, pairs), pl.ds(end * cols, cols)] = out.astype(out_ref.dtype)


def unpack(core, place, mine, theirs):
    group, rows, cols = mine.shape
    block = pl.BlockSpec((1, rows, cols), lambda i, core: (i, 0, 0))
    pairs = place.shape[0] * place.shape[1]
    return pl.pallas_call(
        unpack_kernel,
        grid_spec=pltpu.PrefetchScalarGridSpec(
            num_scalar_prefetch=1,
            grid=(group,),
            in_specs=[pl.BlockSpec(place.shape, lambda i, core: (0, 0, 0)), block, block],
            out_specs=pl.BlockSpec((pairs, 2 * cols), lambda i, core: (0, i)),
        ),
        out_shape=jax.ShapeDtypeStruct((pairs, 2 * group * cols), mine.dtype),
        cost_estimate=pl.CostEstimate(
            flops=4 * pairs * rows * group * cols,
            bytes_accessed=4 * group * cols * (2 * rows + pairs),
            transcendentals=0,
        ),
        name="unpack_rows",
    )(core.reshape(1), place, mine, theirs)


def local(pooled, weight, cotangent, owners, local_rows, table, accum):
    group, hashes = lax.axis_size("group"), lax.axis_size("hash")
    me = lax.axis_index("hash")
    classes = hashes // 4
    my_core = me & 1
    every = range(hashes)

    def far(value, step):
        return lax.ppermute(value, "hash", [(i, (i + 4 * step) % hashes) for i in every])

    def all_far(value):
        return [far(value, step) for step in range(1, classes)]

    def flip(value, bit):
        return lax.ppermute(value, "hash", [(i, i ^ bit) for i in every])

    vectors = pooled[0]
    samples, feats, width = vectors.shape
    feats_local, rows_dev = accum.shape
    early = 3 * samples // 8

    ids = jnp.swapaxes(owners[0] * rows_dev + local_rows[0], 1, 2)
    id_sets = jnp.stack([ids] + all_far(ids))
    early_vectors = all_far(vectors[:early])

    inter = jnp.einsum("sfe,sge->sfg", vectors, vectors, preferred_element_type=jnp.float32).astype(
        jnp.bfloat16
    )
    inter_rows = inter.reshape(samples, feats * feats)
    preact = jnp.dot(inter_rows, weight, preferred_element_type=jnp.float32)
    sigmoid_v = jax.nn.sigmoid(preact)
    dpre = (
        cotangent[0].astype(jnp.float32) * (sigmoid_v * (1.0 + preact * (1.0 - sigmoid_v)))
    ).astype(jnp.bfloat16)
    pairs = pair_table(feats)
    source = jnp.asarray(pairs, jnp.int32)
    pick = (jnp.arange(feats * feats, dtype=jnp.int32)[:, None] == source[None, :]).astype(jnp.bfloat16)
    packed = jnp.dot(inter_rows, pick, preferred_element_type=jnp.float32).astype(jnp.bfloat16)
    parts = jnp.swapaxes(dpre.reshape(samples, group, -1), 0, 1)
    both = jnp.concatenate([jnp.broadcast_to(packed[None], (group,) + packed.shape), parts], axis=2)
    both = lax.all_to_all(both, "group", 0, 0).reshape(group * samples, -1)
    packed_all, dpre_part = both[:, : len(pairs)], both[:, len(pairs) :]

    dinter = lax.dot_general(
        dpre, weight, (((1,), (1,)), ((), ())), preferred_element_type=jnp.float32
    ).reshape(samples, feats, feats)
    id_sets = jnp.stack([id_sets, flip(id_sets, 1)])
    dsym = (dinter + jnp.swapaxes(dinter, 1, 2)).astype(jnp.bfloat16)
    early_dsym = all_far(dsym[:early].reshape(early, feats * feats))
    early_dsym = [sym.reshape(early, feats, feats) for sym in early_dsym]

    def gradients(sym, vecs):
        out = jnp.einsum("sfg,sge->fse", sym, vecs, preferred_element_type=jnp.float32)
        return out.astype(jnp.bfloat16).reshape(group, feats_local, -1, width)

    dpooled = gradients(dsym, vectors)

    sizes = chunk_sizes(feats_local)
    piece_feats = feats_local // 2
    pieces, nears = [], []
    for number in range(2):
        piece = dpooled[:, number * piece_feats : (number + 1) * piece_feats]
        pieces.append(lax.all_to_all(piece, "group", 0, 0))
        nears.append(flip(pieces[-1], 1))
    early_grads = [gradients(sym, vecs) for sym, vecs in zip(early_dsym, early_vectors)]
    early_grads = [lax.all_to_all(value, "group", 0, 0) for value in early_grads]
    early_nears = [flip(value, 1) for value in early_grads]

    targets = jnp.stack([me, me ^ 2]).reshape(2, 1, 1, 1, 1, 1)
    offset = id_sets[None] - targets * rows_dev
    inside = (offset >= 0) & (offset < rows_dev)
    rows_named = jnp.max(jnp.where(inside, offset, -1), axis=4)
    rows_named = jnp.moveaxis(rows_named, 3, 1)
    rows_named = rows_named.reshape(2, feats_local, 2, classes, group, samples)
    rows_far = rows_named[:, :, :, 1:]
    rows_far = [part.reshape(part.shape[:4] + (-1,)) for part in (rows_far[..., :early], rows_far[..., early:])]
    rows_own = rows_named[:, :, :, :1].reshape(2, feats_local, 2, 1, group * samples)
    keys = jnp.concatenate([rows_own, jnp.concatenate(rows_far, axis=-1)], axis=3)
    keys = keys.reshape(2, feats_local, 2 * classes, group * samples)

    def rounded(value):
        return value.astype(jnp.bfloat16)

    def split(value, low, axis):
        a, b = jnp.split(value, 2, axis=axis)
        return jnp.where(low, a, b), jnp.where(low, b, a)

    first_core = my_core == 0
    wsum = lax.dot_general(
        packed_all, dpre_part, (((0,), (0,)), ((), ())), preferred_element_type=jnp.float32
    )
    keep, send = split(wsum, first_core, 1)
    wsum = keep + flip(rounded(send), 1)
    chips = hashes // 2
    my_chip = me >> 1

    def along(value, step):
        return lax.ppermute(value, "hash", [(i, (i + 2 * step) % hashes) for i in every])

    by_chip = wsum.reshape(chips, -1, wsum.shape[1])
    sends = [
        rounded(lax.dynamic_index_in_dim(by_chip, (my_chip + step) % chips, 0, keepdims=False))
        for step in range(1, chips)
    ]
    sends = [along(value, step) for step, value in enumerate(sends, 1)]
    wsum = lax.dynamic_index_in_dim(by_chip, my_chip, 0, keepdims=False)
    for value in sends:
        wsum = wsum + value
    total_samples = samples * group * hashes
    wdone = (wsum / math.sqrt(total_samples)).astype(jnp.bfloat16)
    by_step = jnp.stack([wdone] + [along(wdone, step) for step in range(1, chips)])
    ordered = [
        lax.dynamic_index_in_dim(by_step, (my_chip - number) % chips, 0, keepdims=False)
        for number in range(chips)
    ]
    wdone = jnp.concatenate(ordered, axis=0)
    wdone = lax.all_to_all(jnp.broadcast_to(wdone[None], (group,) + wdone.shape), "group", 0, 0)
    wother = flip(wdone, 1)
    depth = feats * feats // 4 + (len(pairs) - feats * feats // 4) // 2
    full_id = jnp.arange(feats * feats, dtype=jnp.int32).reshape(2, -1, 1)
    row_f, row_g = full_id // feats, full_id % feats
    full_id = jnp.minimum(row_f, row_g) * feats + jnp.maximum(row_f, row_g)
    held = jnp.stack([source[:depth], source[len(pairs) - depth :]])[:, None, :]
    place = (full_id == held).astype(jnp.bfloat16)
    if wdone.shape[2] % 128 == 0:
        wgrad = unpack(my_core, place, wdone, wother)
    else:
        ends = [jnp.where(first_core, wdone, wother), jnp.where(first_core, wother, wdone)]
        wrows = jnp.moveaxis(jnp.concatenate(ends, axis=2), 0, 1).reshape(len(pairs), -1)
        wrows = jnp.stack([wrows[:depth], wrows[len(pairs) - depth :]])
        wgrad = jnp.einsum("apk,akn->apn", place, wrows, preferred_element_type=jnp.float32)
        wgrad = wgrad.astype(jnp.bfloat16).reshape(feats * feats, -1)

    steps = range(classes - 1)
    sets = [[0]] + [[2 + 2 * step, 3 + 2 * step] for step in steps]
    sets += [[1]] + [[2 * classes + 2 * step, 2 * classes + 1 + 2 * step] for step in steps]
    owns, others = [], []
    first = 0
    for size in sizes:
        side = first // piece_feats
        start = first - side * piece_feats
        fars = all_far(pieces[side][:, start : start + size, early:])
        swaps = [flip(value, 1) for value in fars]
        operands, starts = [pieces[side], nears[side]], [start, start]
        for grads, late in ((early_grads, fars), (early_nears, swaps)):
            for step in steps:
                operands += [grads[step], late[step]]
                starts += [first, 0]
        own, sib = dense_rows(keys, sets, operands, starts, first, size, rows_dev)
        other = flip(sib, 2)
        owns.append(own)
        others.append(other)
        first += size
    outs, first = None, 0
    for part in (slice(0, -2), slice(-2, -1), slice(-1, None)):
        if not sizes[part]:
            continue
        outs = update(owns[part], others[part], table, accum, first, outs)
        first += sum(sizes[part])
    table_out, accum_out = outs
    return (wgrad, table_out, accum_out)


def solution(mesh):
    in_specs = (
        P("hash", "group", None, None),
        P(),
        P("hash", "group", None),
        P("hash", "group", None, None),
        P("hash", "group", None, None),
        P("group", "hash", None),
        P("group", "hash"),
    )
    out_specs = (P(), P("group", "hash", None), P("group", "hash"))

    def run(pooled, *others):
        step = jax.shard_map(local, mesh=mesh, in_specs=in_specs, out_specs=out_specs, check_vma=False)
        return step(pooled, *others)

    return run
```

```python
import functools
import math

import jax
import jax.numpy as jnp
from jax import lax
from jax.experimental import pallas as pl
from jax.experimental.pallas import tpu as pltpu
from jax.sharding import PartitionSpec as P


def chunk_sizes(feats_local):
    if feats_local < 4 or feats_local % 4:
        return [1] * feats_local
    return [feats_local // 4] * 4


def pair_table(feats):
    half = feats // 2
    first = [f * feats + g for f in range(half) for g in range(f, half)]
    second = [f * feats + g for f in range(half, feats) for g in range(f, feats)]
    mixed = [f * feats + g for f in range(half) for g in range(half, feats)]
    spare = [-1] * (-len(first) % 16)
    return first + spare + mixed + spare + second


def rows_kernel(sets, keys_ref, *refs):
    vec_refs, (own_ref, sib_ref) = refs[:-2], refs[-2:]
    rows, width = own_ref.shape[1:]
    samples = keys_ref.shape[-1]
    row_id = lax.broadcasted_iota(jnp.int32, (rows, samples), 0)
    vectors = [
        jnp.concatenate([vec_refs[i][:, 0].reshape(-1, width) for i in members], axis=0) for members in sets
    ]
    for target, out_ref in enumerate((own_ref, sib_ref)):
        total = jnp.zeros((rows, width), jnp.float32)
        for line, vec in enumerate(vectors):
            key = keys_ref[target, 0, line : line + 1, :]
            hit = jnp.where(row_id == key, 1.0, 0.0).astype(jnp.bfloat16)
            total = total + jnp.dot(hit, vec, preferred_element_type=jnp.float32)
        out_ref[0] = total.astype(out_ref.dtype)


def dense_rows(keys, sets, vectors, starts, first, feats, rows):
    width = vectors[0].shape[-1]

    def vec_spec(value, start):
        return pl.BlockSpec((value.shape[0], 1) + value.shape[2:], lambda f: (0, start + f, 0, 0))

    key_spec = pl.BlockSpec((2, 1) + keys.shape[2:], lambda f: (0, first + f, 0, 0))
    out_spec = pl.BlockSpec((1, rows, width), lambda f: (f, 0, 0))
    samples = keys.shape[2] * keys.shape[3]
    return pl.pallas_call(
        functools.partial(rows_kernel, sets),
        grid=(feats,),
        in_specs=[key_spec] + [vec_spec(value, start) for value, start in zip(vectors, starts)],
        out_specs=[out_spec, out_spec],
        out_shape=[
            jax.ShapeDtypeStruct((feats, rows, width), jnp.float32),
            jax.ShapeDtypeStruct((feats, rows, width), jnp.bfloat16),
        ],
        cost_estimate=pl.CostEstimate(
            flops=4 * feats * rows * samples * width,
            bytes_accessed=feats * width * (2 * samples + 6 * rows),
            transcendentals=0,
        ),
        name="dense_rows",
    )(keys, *vectors)


def update_kernel(sizes, first, *refs):
    count = len(sizes)
    own_refs, other_refs = refs[:count], refs[count : 2 * count]
    table_ref, accum_ref, before_ref = refs[2 * count : 2 * count + 3]
    table_out, accum_out = refs[-2:]
    rows, width = table_ref.shape[1:]
    lanes = 128
    step = pl.program_id(0)

    @pl.when(step == 0)
    def _():
        accum_out[...] = before_ref[...]

    def one(own_ref, other_ref):
        grad = own_ref[0] + other_ref[0].astype(jnp.float32)
        square = grad * grad
        part = square[:, :lanes]
        for start in range(lanes, width, lanes):
            part = part + square[:, start : start + lanes]
        mean = jnp.sum(part.T, axis=0, keepdims=True) * (1.0 / width)
        line = pl.ds(first + step, 1)
        state = accum_ref[line, :] + mean
        accum_out[line, :] = state
        scale = jnp.broadcast_to(0.1 / jnp.sqrt(state), (lanes, rows)).T
        for start in range(0, width, lanes):
            window = pl.ds(start, lanes)
            table_out[0, :, window] = table_ref[0, :, window] - grad[:, start : start + lanes] * scale

    low = 0
    for size, own_ref, other_ref in zip(sizes, own_refs, other_refs):
        pl.when((step >= low) & (step < low + size))(functools.partial(one, own_ref, other_ref))
        low += size


def update(owns, others, table, accum, first, before):
    sizes = [own.shape[0] for own in owns]
    rows, width = owns[0].shape[1:]
    feats = sum(sizes)

    def part(low, size):
        return pl.BlockSpec((1, rows, width), lambda f: (jnp.clip(f - low, 0, size - 1), 0, 0))

    parts, low = [], 0
    for size in sizes:
        parts.append(part(low, size))
        low += size
    whole = pl.BlockSpec((1, rows, width), lambda f: (first + f, 0, 0))
    lines = pl.BlockSpec(accum.shape, lambda f: (0, 0))
    extra = [] if before is None else [before[0]]
    return pl.pallas_call(
        functools.partial(update_kernel, sizes, first),
        grid=(feats,),
        in_specs=parts + parts + [whole, lines, lines] + [pl.BlockSpec(memory_space=pl.ANY)] * len(extra),
        out_specs=[whole, lines],
        out_shape=[
            jax.ShapeDtypeStruct(table.shape, table.dtype),
            jax.ShapeDtypeStruct(accum.shape, accum.dtype),
        ],
        input_output_aliases={2 * len(owns) + 3: 0} if extra else {},
        cost_estimate=pl.CostEstimate(
            flops=8 * feats * rows * width,
            bytes_accessed=14 * feats * rows * width,
            transcendentals=feats * rows,
        ),
        name="update_rows",
    )(*owns, *others, table, accum, accum if before is None else before[1], *extra)


def unpack_kernel(core_ref, place_ref, mine_ref, theirs_ref, out_ref):
    parts, pairs, depth = place_ref.shape
    rows, cols = mine_ref.shape[1:]
    low = core_ref[0] == 0
    mine, theirs = mine_ref[0], theirs_ref[0]
    for end, block in enumerate((jnp.where(low, mine, theirs), jnp.where(low, theirs, mine))):
        for part in range(parts):
            start = part * (rows - depth)
            out = jnp.dot(
                place_ref[part], block[start : start + depth], preferred_element_type=jnp.float32
            )
            out_ref[pl.ds(part * pairs, pairs), pl.ds(end * cols, cols)] = out.astype(out_ref.dtype)


def unpack(core, place, mine, theirs):
    group, rows, cols = mine.shape
    block = pl.BlockSpec((1, rows, cols), lambda i, core: (i, 0, 0))
    pairs = place.shape[0] * place.shape[1]
    return pl.pallas_call(
        unpack_kernel,
        grid_spec=pltpu.PrefetchScalarGridSpec(
            num_scalar_prefetch=1,
            grid=(group,),
            in_specs=[pl.BlockSpec(place.shape, lambda i, core: (0, 0, 0)), block, block],
            out_specs=pl.BlockSpec((pairs, 2 * cols), lambda i, core: (0, i)),
        ),
        out_shape=jax.ShapeDtypeStruct((pairs, 2 * group * cols), mine.dtype),
        cost_estimate=pl.CostEstimate(
            flops=4 * pairs * rows * group * cols,
            bytes_accessed=4 * group * cols * (2 * rows + pairs),
            transcendentals=0,
        ),
        name="unpack_rows",
    )(core.reshape(1), place, mine, theirs)


def local(pooled, weight, cotangent, owners, local_rows, table, accum):
    group, hashes = lax.axis_size("group"), lax.axis_size("hash")
    me = lax.axis_index("hash")
    classes = hashes // 4
    my_core = me & 1
    every = range(hashes)

    def far(value, step):
        return lax.ppermute(value, "hash", [(i, (i + 4 * step) % hashes) for i in every])

    def all_far(value):
        return [far(value, step) for step in range(1, classes)]

    def flip(value, bit):
        return lax.ppermute(value, "hash", [(i, i ^ bit) for i in every])

    vectors = pooled[0]
    samples, feats, width = vectors.shape
    feats_local, rows_dev = accum.shape
    early = 3 * samples // 8

    ids = jnp.swapaxes(owners[0] * rows_dev + local_rows[0], 1, 2)
    id_sets = jnp.stack([ids] + all_far(ids))
    early_vectors = all_far(vectors[:early])

    inter = jnp.einsum("sfe,sge->sfg", vectors, vectors, preferred_element_type=jnp.float32).astype(
        jnp.bfloat16
    )
    inter_rows = inter.reshape(samples, feats * feats)
    preact = jnp.dot(inter_rows, weight, preferred_element_type=jnp.float32)
    sigmoid_v = jax.nn.sigmoid(preact)
    dpre = (
        cotangent[0].astype(jnp.float32) * (sigmoid_v * (1.0 + preact * (1.0 - sigmoid_v)))
    ).astype(jnp.bfloat16)
    pairs = pair_table(feats)
    source = jnp.asarray(pairs, jnp.int32)
    pick = (jnp.arange(feats * feats, dtype=jnp.int32)[:, None] == source[None, :]).astype(jnp.bfloat16)
    packed = jnp.dot(inter_rows, pick, preferred_element_type=jnp.float32).astype(jnp.bfloat16)
    parts = jnp.swapaxes(dpre.reshape(samples, group, -1), 0, 1)
    both = jnp.concatenate([jnp.broadcast_to(packed[None], (group,) + packed.shape), parts], axis=2)
    both = lax.all_to_all(both, "group", 0, 0).reshape(group * samples, -1)
    packed_all, dpre_part = both[:, : len(pairs)], both[:, len(pairs) :]

    dinter = lax.dot_general(
        dpre, weight, (((1,), (1,)), ((), ())), preferred_element_type=jnp.float32
    ).reshape(samples, feats, feats)
    id_sets = jnp.stack([id_sets, flip(id_sets, 1)])
    dsym = (dinter + jnp.swapaxes(dinter, 1, 2)).astype(jnp.bfloat16)
    early_dsym = all_far(dsym[:early].reshape(early, feats * feats))
    early_dsym = [sym.reshape(early, feats, feats) for sym in early_dsym]

    def gradients(sym, vecs):
        out = jnp.einsum("sfg,sge->fse", sym, vecs, preferred_element_type=jnp.float32)
        return out.astype(jnp.bfloat16).reshape(group, feats_local, -1, width)

    dpooled = gradients(dsym, vectors)

    sizes = chunk_sizes(feats_local)
    piece_feats = feats_local // 2
    pieces, nears = [], []
    for number in range(2):
        piece = dpooled[:, number * piece_feats : (number + 1) * piece_feats]
        pieces.append(lax.all_to_all(piece, "group", 0, 0))
        nears.append(flip(pieces[-1], 1))
    early_grads = [gradients(sym, vecs) for sym, vecs in zip(early_dsym, early_vectors)]
    early_grads = [lax.all_to_all(value, "group", 0, 0) for value in early_grads]
    early_nears = [flip(value, 1) for value in early_grads]

    targets = jnp.stack([me, me ^ 2]).reshape(2, 1, 1, 1, 1, 1)
    offset = id_sets[None] - targets * rows_dev
    inside = (offset >= 0) & (offset < rows_dev)
    rows_named = jnp.max(jnp.where(inside, offset, -1), axis=4)
    rows_named = jnp.moveaxis(rows_named, 3, 1)
    rows_named = rows_named.reshape(2, feats_local, 2, classes, group, samples)
    rows_far = rows_named[:, :, :, 1:]
    rows_far = [part.reshape(part.shape[:4] + (-1,)) for part in (rows_far[..., :early], rows_far[..., early:])]
    rows_own = rows_named[:, :, :, :1].reshape(2, feats_local, 2, 1, group * samples)
    keys = jnp.concatenate([rows_own, jnp.concatenate(rows_far, axis=-1)], axis=3)
    keys = keys.reshape(2, feats_local, 2 * classes, group * samples)

    def rounded(value):
        return value.astype(jnp.bfloat16)

    def split(value, low, axis):
        a, b = jnp.split(value, 2, axis=axis)
        return jnp.where(low, a, b), jnp.where(low, b, a)

    first_core = my_core == 0
    wsum = lax.dot_general(
        packed_all, dpre_part, (((0,), (0,)), ((), ())), preferred_element_type=jnp.float32
    )
    keep, send = split(wsum, first_core, 1)
    send = flip(rounded(send), 1)
    wsum = keep + send
    chips = hashes // 2
    my_chip = me >> 1

    def along(value, step):
        return lax.ppermute(value, "hash", [(i, (i + 2 * step) % hashes) for i in every])

    by_chip = wsum.reshape(chips, -1, wsum.shape[1])
    sends = [
        rounded(lax.dynamic_index_in_dim(by_chip, lax.rem(my_chip + step, chips), 0, keepdims=False))
        for step in range(1, chips)
    ]
    sends = [along(value, step) for step, value in enumerate(sends, 1)]
    wsum = lax.dynamic_index_in_dim(by_chip, my_chip, 0, keepdims=False)
    for value in sends:
        wsum = wsum + value
    total_samples = samples * group * hashes
    wdone = (wsum / math.sqrt(total_samples)).astype(jnp.bfloat16)
    by_step = jnp.stack([wdone] + [along(wdone, step) for step in range(1, chips)])
    ordered = [
        lax.dynamic_index_in_dim(by_step, lax.rem(my_chip + chips - number, chips), 0, keepdims=False)
        for number in range(chips)
    ]
    wdone = jnp.concatenate(ordered, axis=0)
    wdone = lax.all_to_all(jnp.broadcast_to(wdone[None], (group,) + wdone.shape), "group", 0, 0)
    wother = flip(wdone, 1)
    depth = feats * feats // 4 + (len(pairs) - feats * feats // 4) // 2
    full_id = jnp.arange(feats * feats, dtype=jnp.int32).reshape(2, -1, 1)
    row_f, row_g = full_id // feats, full_id % feats
    full_id = jnp.minimum(row_f, row_g) * feats + jnp.maximum(row_f, row_g)
    held = jnp.stack([source[:depth], source[len(pairs) - depth :]])[:, None, :]
    place = (full_id == held).astype(jnp.bfloat16)
    if wdone.shape[2] % 128 == 0:
        wgrad = unpack(my_core, place, wdone, wother)
    else:
        ends = [jnp.where(first_core, wdone, wother), jnp.where(first_core, wother, wdone)]
        wrows = jnp.moveaxis(jnp.concatenate(ends, axis=2), 0, 1).reshape(len(pairs), -1)
        wrows = jnp.stack([wrows[:depth], wrows[len(pairs) - depth :]])
        wgrad = jnp.einsum("apk,akn->apn", place, wrows, preferred_element_type=jnp.float32)
        wgrad = wgrad.astype(jnp.bfloat16).reshape(feats * feats, -1)

    steps = range(classes - 1)
    sets = [[0]] + [[2 + 2 * step, 3 + 2 * step] for step in steps]
    sets += [[1]] + [[2 * classes + 2 * step, 2 * classes + 1 + 2 * step] for step in steps]
    owns, others = [], []
    first = 0
    for size in sizes:
        side = first // piece_feats
        start = first - side * piece_feats
        fars = all_far(pieces[side][:, start : start + size, early:])
        swaps = [flip(value, 1) for value in fars]
        operands, starts = [pieces[side], nears[side]], [start, start]
        for grads, late in ((early_grads, fars), (early_nears, swaps)):
            for step in steps:
                operands += [grads[step], late[step]]
                starts += [first, 0]
        own, sib = dense_rows(keys, sets, operands, starts, first, size, rows_dev)
        other = flip(sib, 2)
        owns.append(own)
        others.append(other)
        first += size
    outs, first = None, 0
    for number, size in enumerate(sizes):
        outs = update([owns[number]], [others[number]], table, accum, first, outs)
        first += size
    table_out, accum_out = outs
    return (wgrad, table_out, accum_out)


def solution(mesh):
    in_specs = (
        P("hash", "group", None, None),
        P(),
        P("hash", "group", None),
        P("hash", "group", None, None),
        P("hash", "group", None, None),
        P("group", "hash", None),
        P("group", "hash"),
    )
    out_specs = (P(), P("group", "hash", None), P("group", "hash"))

    def run(pooled, *others):
        step = jax.shard_map(local, mesh=mesh, in_specs=in_specs, out_specs=out_specs, check_vma=False)
        return step(pooled, *others)

    return run
```

```python
import functools
import math

import jax
import jax.numpy as jnp
from jax import lax
from jax.experimental import pallas as pl
from jax.experimental.pallas import tpu as pltpu
from jax.sharding import PartitionSpec as P


def chunk_sizes(feats_local):
    if feats_local < 4 or feats_local % 4:
        return [1] * feats_local
    return [feats_local // 4] * 4


def pair_table(feats):
    half = feats // 2
    first = [f * feats + g for f in range(half) for g in range(f, half)]
    second = [f * feats + g for f in range(half, feats) for g in range(f, feats)]
    mixed = [f * feats + g for f in range(half) for g in range(half, feats)]
    spare = [-1] * (-len(first) % 16)
    return first + spare + mixed + spare + second


def rows_kernel(sets, keys_ref, *refs):
    vec_refs, (own_ref, sib_ref) = refs[:-2], refs[-2:]
    rows, width = own_ref.shape[1:]
    samples = keys_ref.shape[-1]
    row_id = lax.broadcasted_iota(jnp.int32, (rows, samples), 0)
    vectors = [
        jnp.concatenate([vec_refs[i][:, 0].reshape(-1, width) for i in members], axis=0) for members in sets
    ]
    for target, out_ref in enumerate((own_ref, sib_ref)):
        total = jnp.zeros((rows, width), jnp.float32)
        for line, vec in enumerate(vectors):
            key = keys_ref[target, 0, line : line + 1, :]
            hit = jnp.where(row_id == key, 1.0, 0.0).astype(jnp.bfloat16)
            total = total + jnp.dot(hit, vec, preferred_element_type=jnp.float32)
        out_ref[0] = total.astype(out_ref.dtype)


def dense_rows(keys, sets, vectors, starts, first, feats, rows):
    width = vectors[0].shape[-1]

    def vec_spec(value, start):
        return pl.BlockSpec((value.shape[0], 1) + value.shape[2:], lambda f: (0, start + f, 0, 0))

    key_spec = pl.BlockSpec((2, 1) + keys.shape[2:], lambda f: (0, first + f, 0, 0))
    out_spec = pl.BlockSpec((1, rows, width), lambda f: (f, 0, 0))
    samples = keys.shape[2] * keys.shape[3]
    return pl.pallas_call(
        functools.partial(rows_kernel, sets),
        grid=(feats,),
        in_specs=[key_spec] + [vec_spec(value, start) for value, start in zip(vectors, starts)],
        out_specs=[out_spec, out_spec],
        out_shape=[
            jax.ShapeDtypeStruct((feats, rows, width), jnp.float32),
            jax.ShapeDtypeStruct((feats, rows, width), jnp.bfloat16),
        ],
        cost_estimate=pl.CostEstimate(
            flops=4 * feats * rows * samples * width,
            bytes_accessed=feats * width * (2 * samples + 6 * rows),
            transcendentals=0,
        ),
        name="dense_rows",
    )(keys, *vectors)


def update_kernel(sizes, first, *refs):
    count = len(sizes)
    own_refs, other_refs = refs[:count], refs[count : 2 * count]
    table_ref, accum_ref, before_ref = refs[2 * count : 2 * count + 3]
    table_out, accum_out = refs[-2:]
    rows, width = table_ref.shape[1:]
    lanes = 128
    step = pl.program_id(0)

    @pl.when(step == 0)
    def _():
        accum_out[...] = before_ref[...]

    def one(own_ref, other_ref):
        grad = own_ref[0] + other_ref[0].astype(jnp.float32)
        square = grad * grad
        part = square[:, :lanes]
        for start in range(lanes, width, lanes):
            part = part + square[:, start : start + lanes]
        mean = jnp.sum(part.T, axis=0, keepdims=True) * (1.0 / width)
        line = pl.ds(first + step, 1)
        state = accum_ref[line, :] + mean
        accum_out[line, :] = state
        scale = jnp.broadcast_to(0.1 / jnp.sqrt(state), (lanes, rows)).T
        for start in range(0, width, lanes):
            window = pl.ds(start, lanes)
            table_out[0, :, window] = table_ref[0, :, window] - grad[:, start : start + lanes] * scale

    low = 0
    for size, own_ref, other_ref in zip(sizes, own_refs, other_refs):
        pl.when((step >= low) & (step < low + size))(functools.partial(one, own_ref, other_ref))
        low += size


def update(owns, others, table, accum, first, before):
    sizes = [own.shape[0] for own in owns]
    rows, width = owns[0].shape[1:]
    feats = sum(sizes)

    def part(low, size):
        return pl.BlockSpec((1, rows, width), lambda f: (jnp.clip(f - low, 0, size - 1), 0, 0))

    parts, low = [], 0
    for size in sizes:
        parts.append(part(low, size))
        low += size
    whole = pl.BlockSpec((1, rows, width), lambda f: (first + f, 0, 0))
    lines = pl.BlockSpec(accum.shape, lambda f: (0, 0))
    extra = [] if before is None else [before[0]]
    return pl.pallas_call(
        functools.partial(update_kernel, sizes, first),
        grid=(feats,),
        in_specs=parts + parts + [whole, lines, lines] + [pl.BlockSpec(memory_space=pl.ANY)] * len(extra),
        out_specs=[whole, lines],
        out_shape=[
            jax.ShapeDtypeStruct(table.shape, table.dtype),
            jax.ShapeDtypeStruct(accum.shape, accum.dtype),
        ],
        input_output_aliases={2 * len(owns) + 3: 0} if extra else {},
        cost_estimate=pl.CostEstimate(
            flops=8 * feats * rows * width,
            bytes_accessed=14 * feats * rows * width,
            transcendentals=feats * rows,
        ),
        name="update_rows",
    )(*owns, *others, table, accum, accum if before is None else before[1], *extra)


def unpack_kernel(core_ref, place_ref, mine_ref, theirs_ref, out_ref):
    parts, pairs, depth = place_ref.shape
    rows, cols = mine_ref.shape[1:]
    low = core_ref[0] == 0
    mine, theirs = mine_ref[0], theirs_ref[0]
    for end, block in enumerate((jnp.where(low, mine, theirs), jnp.where(low, theirs, mine))):
        for part in range(parts):
            start = part * (rows - depth)
            out = jnp.dot(
                place_ref[part], block[start : start + depth], preferred_element_type=jnp.float32
            )
            out_ref[pl.ds(part * pairs, pairs), pl.ds(end * cols, cols)] = out.astype(out_ref.dtype)


def unpack(core, place, mine, theirs):
    group, rows, cols = mine.shape
    block = pl.BlockSpec((1, rows, cols), lambda i, core: (i, 0, 0))
    pairs = place.shape[0] * place.shape[1]
    return pl.pallas_call(
        unpack_kernel,
        grid_spec=pltpu.PrefetchScalarGridSpec(
            num_scalar_prefetch=1,
            grid=(group,),
            in_specs=[pl.BlockSpec(place.shape, lambda i, core: (0, 0, 0)), block, block],
            out_specs=pl.BlockSpec((pairs, 2 * cols), lambda i, core: (0, i)),
        ),
        out_shape=jax.ShapeDtypeStruct((pairs, 2 * group * cols), mine.dtype),
        cost_estimate=pl.CostEstimate(
            flops=4 * pairs * rows * group * cols,
            bytes_accessed=4 * group * cols * (2 * rows + pairs),
            transcendentals=0,
        ),
        name="unpack_rows",
    )(core.reshape(1), place, mine, theirs)


def local(pooled, weight, cotangent, owners, local_rows, table, accum):
    group, hashes = lax.axis_size("group"), lax.axis_size("hash")
    me = lax.axis_index("hash")
    classes = hashes // 4
    my_core = me & 1
    every = range(hashes)

    def far(value, step):
        return lax.ppermute(value, "hash", [(i, (i + 4 * step) % hashes) for i in every])

    def all_far(value):
        return [far(value, step) for step in range(1, classes)]

    def flip(value, bit):
        return lax.ppermute(value, "hash", [(i, i ^ bit) for i in every])

    vectors = pooled[0]
    samples, feats, width = vectors.shape
    feats_local, rows_dev = accum.shape
    early = 3 * samples // 8

    ids = jnp.swapaxes(owners[0] * rows_dev + local_rows[0], 1, 2)
    id_sets = jnp.stack([ids] + all_far(ids))
    early_vectors = all_far(vectors[:early])

    inter = jnp.einsum("sfe,sge->sfg", vectors, vectors, preferred_element_type=jnp.float32).astype(
        jnp.bfloat16
    )
    inter_rows = inter.reshape(samples, feats * feats)
    preact = jnp.dot(inter_rows, weight, preferred_element_type=jnp.float32)
    sigmoid_v = jax.nn.sigmoid(preact)
    dpre = (
        cotangent[0].astype(jnp.float32) * (sigmoid_v * (1.0 + preact * (1.0 - sigmoid_v)))
    ).astype(jnp.bfloat16)
    pairs = pair_table(feats)
    source = jnp.asarray(pairs, jnp.int32)
    pick = (jnp.arange(feats * feats, dtype=jnp.int32)[:, None] == source[None, :]).astype(jnp.bfloat16)
    packed = jnp.dot(inter_rows, pick, preferred_element_type=jnp.float32).astype(jnp.bfloat16)
    parts = jnp.swapaxes(dpre.reshape(samples, group, -1), 0, 1)
    both = jnp.concatenate([jnp.broadcast_to(packed[None], (group,) + packed.shape), parts], axis=2)
    both = lax.all_to_all(both, "group", 0, 0).reshape(group * samples, -1)
    packed_all, dpre_part = both[:, : len(pairs)], both[:, len(pairs) :]

    dinter = lax.dot_general(
        dpre, weight, (((1,), (1,)), ((), ())), preferred_element_type=jnp.float32
    ).reshape(samples, feats, feats)
    id_sets = jnp.stack([id_sets, flip(id_sets, 1)])
    dsym = (dinter + jnp.swapaxes(dinter, 1, 2)).astype(jnp.bfloat16)
    early_dsym = all_far(dsym[:early].reshape(early, feats * feats))
    early_dsym = [sym.reshape(early, feats, feats) for sym in early_dsym]

    def gradients(sym, vecs):
        out = jnp.einsum("sfg,sge->fse", sym, vecs, preferred_element_type=jnp.float32)
        return out.astype(jnp.bfloat16).reshape(group, feats_local, -1, width)

    dpooled = gradients(dsym, vectors)

    sizes = chunk_sizes(feats_local)
    piece_feats = feats_local // 2
    pieces, nears = [], []
    for number in range(2):
        piece = dpooled[:, number * piece_feats : (number + 1) * piece_feats]
        pieces.append(lax.all_to_all(piece, "group", 0, 0))
        nears.append(flip(pieces[-1], 1))
    early_grads = [gradients(sym, vecs) for sym, vecs in zip(early_dsym, early_vectors)]
    early_grads = [lax.all_to_all(value, "group", 0, 0) for value in early_grads]
    early_nears = [flip(value, 1) for value in early_grads]

    targets = jnp.stack([me, me ^ 2]).reshape(2, 1, 1, 1, 1, 1)
    offset = id_sets[None] - targets * rows_dev
    inside = (offset >= 0) & (offset < rows_dev)
    rows_named = jnp.max(jnp.where(inside, offset, -1), axis=4)
    rows_named = jnp.moveaxis(rows_named, 3, 1)
    rows_named = rows_named.reshape(2, feats_local, 2, classes, group, samples)
    rows_far = rows_named[:, :, :, 1:]
    rows_far = [part.reshape(part.shape[:4] + (-1,)) for part in (rows_far[..., :early], rows_far[..., early:])]
    rows_own = rows_named[:, :, :, :1].reshape(2, feats_local, 2, 1, group * samples)
    keys = jnp.concatenate([rows_own, jnp.concatenate(rows_far, axis=-1)], axis=3)
    keys = keys.reshape(2, feats_local, 2 * classes, group * samples)

    def rounded(value):
        return value.astype(jnp.bfloat16)

    def split(value, low, axis):
        a, b = jnp.split(value, 2, axis=axis)
        return jnp.where(low, a, b), jnp.where(low, b, a)

    first_core = my_core == 0
    wsum = lax.dot_general(
        packed_all, dpre_part, (((0,), (0,)), ((), ())), preferred_element_type=jnp.float32
    )
    keep, send = split(wsum, first_core, 1)
    send = flip(rounded(send), 1)
    wsum = keep + send
    chips = hashes // 2
    my_chip = me >> 1

    def along(value, step):
        return lax.ppermute(value, "hash", [(i, (i + 2 * step) % hashes) for i in every])

    by_chip = wsum.reshape(chips, -1, wsum.shape[1])
    sends = [
        rounded(lax.dynamic_index_in_dim(by_chip, lax.rem(my_chip + step, chips), 0, keepdims=False))
        for step in range(1, chips)
    ]
    sends = [along(value, step) for step, value in enumerate(sends, 1)]
    wsum = lax.dynamic_index_in_dim(by_chip, my_chip, 0, keepdims=False)
    for value in sends:
        wsum = wsum + value
    total_samples = samples * group * hashes
    wdone = (wsum / math.sqrt(total_samples)).astype(jnp.bfloat16)
    by_step = jnp.stack([wdone] + [along(wdone, step) for step in range(1, chips)])
    ordered = [
        lax.dynamic_index_in_dim(by_step, lax.rem(my_chip + chips - number, chips), 0, keepdims=False)
        for number in range(chips)
    ]
    wdone = jnp.concatenate(ordered, axis=0)
    wdone = lax.all_to_all(jnp.broadcast_to(wdone[None], (group,) + wdone.shape), "group", 0, 0)
    wother = flip(wdone, 1)
    depth = feats * feats // 4 + (len(pairs) - feats * feats // 4) // 2
    full_id = jnp.arange(feats * feats, dtype=jnp.int32).reshape(2, -1, 1)
    row_f, row_g = full_id // feats, full_id % feats
    full_id = jnp.minimum(row_f, row_g) * feats + jnp.maximum(row_f, row_g)
    held = jnp.stack([source[:depth], source[len(pairs) - depth :]])[:, None, :]
    place = (full_id == held).astype(jnp.bfloat16)
    if wdone.shape[2] % 128 == 0:
        wgrad = unpack(my_core, place, wdone, wother)
    else:
        ends = [jnp.where(first_core, wdone, wother), jnp.where(first_core, wother, wdone)]
        wrows = jnp.moveaxis(jnp.concatenate(ends, axis=2), 0, 1).reshape(len(pairs), -1)
        wrows = jnp.stack([wrows[:depth], wrows[len(pairs) - depth :]])
        wgrad = jnp.einsum("apk,akn->apn", place, wrows, preferred_element_type=jnp.float32)
        wgrad = wgrad.astype(jnp.bfloat16).reshape(feats * feats, -1)

    steps = range(classes - 1)
    sets = [[0]] + [[2 + 2 * step, 3 + 2 * step] for step in steps]
    sets += [[1]] + [[2 * classes + 2 * step, 2 * classes + 1 + 2 * step] for step in steps]
    owns, others = [], []
    first = 0
    for size in sizes:
        side = first // piece_feats
        start = first - side * piece_feats
        fars = all_far(pieces[side][:, start : start + size, early:])
        swaps = [flip(value, 1) for value in fars]
        operands, starts = [pieces[side], nears[side]], [start, start]
        for grads, late in ((early_grads, fars), (early_nears, swaps)):
            for step in steps:
                operands += [grads[step], late[step]]
                starts += [first, 0]
        own, sib = dense_rows(keys, sets, operands, starts, first, size, rows_dev)
        other = flip(sib, 2)
        owns.append(own)
        others.append(other)
        first += size
    outs, first = None, 0
    groups = [slice(0, 2)] + [slice(number, number + 1) for number in range(2, len(sizes))]
    for part in groups:
        outs = update(owns[part], others[part], table, accum, first, outs)
        first += sum(sizes[part])
    table_out, accum_out = outs
    return (wgrad, table_out, accum_out)


def solution(mesh):
    in_specs = (
        P("hash", "group", None, None),
        P(),
        P("hash", "group", None),
        P("hash", "group", None, None),
        P("hash", "group", None, None),
        P("group", "hash", None),
        P("group", "hash"),
    )
    out_specs = (P(), P("group", "hash", None), P("group", "hash"))

    def run(pooled, *others):
        step = jax.shard_map(local, mesh=mesh, in_specs=in_specs, out_specs=out_specs, check_vma=False)
        return step(pooled, *others)

    return run
```
